512 devices in a mesh: seq: 128 (over z, y, core), mp: 4 (over x).
Axes of the slice: x: 4, y: 4, z: 16, core: 2. Of those that a mesh axis runs over, the one named last changes fastest.
Arguments:
- queries: bfloat16 [8192, 2048], P('seq', 'mp'), may hold values from -14 to 14
- keys: bfloat16 [8192, 2048], P('seq', 'mp'), may hold values from -14 to 14
- values: bfloat16 [8192, 2048], P('seq', 'mp'), may hold values from -6 to 6
- stream: bfloat16 [8192, 2048], P('seq', 'mp'), may hold values from -6 to 6
- seg_lengths: int32 [64], replicated, may hold values from 1 to 256, 8192 in all
- gain: float32 [2048], replicated, may hold values from 0.5 to 1.5
- w_out: bfloat16 [2048, 2048], P('mp', 'seq'), may hold values from -0.125 to 0.125
- w_gate: bfloat16 [2048, 3072], P('seq', 'mp'), may hold values from -0.125 to 0.125
- w_up: bfloat16 [2048, 3072], P('seq', 'mp'), may hold values from -0.125 to 0.125
- w_down: bfloat16 [3072, 2048], P('mp', 'seq'), may hold values from -0.109375 to 0.109375
Outputs:
- mixed: bfloat16 [8192, 2048], P('seq', 'mp')
The draws below stay inside these ranges and needn't reach their ends.
Inputs may be any that keep to these rules, and one draw needn't show every extreme that they name: `seg_lengths`: the segments of landmarks 0 to 63 follow one another and cover the document's 8192 tokens.
All inputs are finite; a program needn't handle non-finite values.
Results may differ from the reference program's by a relative error of at most 0.014.
Values may be sent and summed in bfloat16 or wider, within the bound.
No kernel may reach another device: no remote copies, remote signals or barrier semaphores. Data moves between devices by JAX's collectives and lax.ppermute only.
A program may use at most 64 MiB of HBM per device.

```python
import math
import jax
import jax.numpy as jnp
import numpy as np
from jax import lax

D = 2048
HEADS = 16
FF = 3072
LANDMARKS = 64
PINV_ITERS = 6
HEAD = 128
TOKENS = 8192
N_MP = 4


def shared_signal(key):
    freqs = jax.random.randint(jax.random.fold_in(key, 11), (D,), 1, 33).astype(jnp.float32)
    phases = jax.random.uniform(jax.random.fold_in(key, 12), (D,), jnp.float32, -math.pi, math.pi)
    place = jnp.arange(TOKENS, dtype=jnp.float32) / TOKENS
    return 1.5 * jnp.sin(2.0 * math.pi * place[:, None] * freqs[None, :] + phases[None, :])


def draw_queries(key, part):
    noise = jnp.clip(jax.random.normal(jax.random.fold_in(key, 1), (TOKENS, D), jnp.float32), -4.0, 4.0)
    result = noise + shared_signal(key)
    return result.astype(jnp.bfloat16)


def draw_keys(key, part):
    noise = jnp.clip(jax.random.normal(jax.random.fold_in(key, 2), (TOKENS, D), jnp.float32), -4.0, 4.0)
    result = noise + shared_signal(key)
    return result.astype(jnp.bfloat16)


def steps_of(own_key, dims, cuts, least, largest):
    def one(position, shards_of):
        draws = jax.random.uniform(jax.random.fold_in(jax.random.fold_in(own_key, 6), position), (shards_of,), jnp.float32, least / len(cuts), largest / len(cuts))
        return jnp.repeat(jnp.exp(draws), dims[position] // shards_of).reshape((-1,) + (1,) * (len(dims) - position - 1))

    level = one(*cuts[0])
    for cut in cuts[1:]:
        level = level * one(*cut)
    return level


def profile(count, total, limit, slope):
    portions = [(1 << 20) // math.isqrt(grade ** slope) + 1 for grade in range(2, count + 1)]
    surplus, holding = total - limit - (count - 1), [1] * (count - 1)
    while surplus > 0:
        free = [i for i in range(count - 1) if holding[i] < limit]
        whole, left = sum([portions[i] for i in free]), surplus
        for i in free:
            more = min(limit - holding[i], max(1, left * portions[i] // whole), surplus)
            holding[i] = holding[i] + more
            surplus = surplus - more
    return np.array([limit] + holding)


def ragged(key, count, total, limit, skew):
    if count == 2:
        one = jax.random.randint(key, (), max(1, total - limit), min(limit, total - 1) + 1)
        return jnp.stack([one, total - one])
    tallies = jnp.asarray(profile(count, total, limit, skew), jnp.int32)
    twos = (count - 1) // 2
    donor, taker = tallies[1:1 + 2 * twos:2], tallies[2:2 + 2 * twos:2]
    slack = jnp.minimum(donor - 1, limit - taker)
    shifted = jax.random.randint(jax.random.fold_in(key, 1), (twos,), 0, 1 << 20) % (slack + 1)
    tallies = tallies.at[1:1 + 2 * twos:2].set(donor - shifted).at[2:2 + 2 * twos:2].set(taker + shifted)
    return tallies[jax.random.permutation(jax.random.fold_in(key, 2), count)]


def bell_draw(rng, shape, width, bound, shards=(), held_as=jnp.bfloat16):
    entries = jax.random.normal(rng, shape, jnp.float32) * width
    if len(shards) > 0:
        entries = steps_of(rng, shape, shards, -0.22, 0.18) * entries
    return jnp.clip(entries, min=-bound, max=bound).astype(held_as)


def setup_inputs(seed: int = 0) -> dict:
    splits = jax.random.split(jax.random.key(seed), 11)
    return {
        "queries": draw_queries(jax.random.fold_in(splits[10], 71), 0),
        "keys": draw_keys(jax.random.fold_in(splits[10], 71), 0),
        "values": bell_draw(splits[2], (TOKENS, D), 1.0, 6.0, ((0, 128), (1, 4))),
        "stream": bell_draw(splits[3], (TOKENS, D), 1.0, 6.0, ((0, 128), (1, 4))),
        "seg_lengths": ragged(splits[4], LANDMARKS, TOKENS, 2 * TOKENS // LANDMARKS, 1).astype(jnp.int32),
        "gain": jnp.clip(1.0 + 0.1 * jax.random.normal(splits[5], (D,), jnp.float32), 0.5, 1.5),
        "w_out": bell_draw(splits[6], (D, D), D ** -0.5, 0.125, ((0, 4), (1, 128))),
        "w_gate": bell_draw(splits[7], (D, FF), D ** -0.5, 0.125, ((0, 128), (1, 4))),
        "w_up": bell_draw(splits[8], (D, FF), D ** -0.5, 0.125, ((0, 128), (1, 4))),
        "w_down": bell_draw(splits[9], (FF, D), FF ** -0.5, 0.109375, ((0, 4), (1, 128))),
    }


HIGH_ACCURACY = lax.Precision.HIGHEST
EPS = 1e-05

def inverse_rounds(anchor_block):
    eye = jnp.eye(anchor_block.shape[0], dtype=jnp.float32)
    col_most = jnp.max(lax.optimization_barrier(jnp.sum(anchor_block, axis=0)))
    row_most = jnp.max(lax.optimization_barrier(jnp.sum(anchor_block, axis=1)))
    approx = anchor_block.T / (col_most * row_most)
    for step in range(PINV_ITERS):
        prod = jnp.dot(anchor_block, approx, precision=HIGH_ACCURACY)
        inner = 7.0 * eye - prod
        inner = 15.0 * eye - jnp.dot(prod, inner, precision=HIGH_ACCURACY)
        inner = 13.0 * eye - jnp.dot(prod, inner, precision=HIGH_ACCURACY)
        approx = 0.25 * jnp.dot(approx, inner, precision=HIGH_ACCURACY)
    return approx

def reference(queries, keys, values, stream, seg_lengths, gain, w_out, w_gate, w_up, w_down):
    ends = jnp.cumsum(seg_lengths).astype(jnp.int32)
    starts = ends - seg_lengths
    place = jnp.arange(TOKENS, dtype=jnp.int32)
    member = ((place[:, None] >= starts[None, :]) & (place[:, None] < ends[None, :])).astype(jnp.bfloat16)
    counts = seg_lengths.astype(jnp.float32)
    query_anchors = jnp.dot(member.T, queries, preferred_element_type=jnp.float32) / counts[:, None]
    key_anchors = jnp.dot(member.T, keys, preferred_element_type=jnp.float32) / counts[:, None]
    score_scale = 1.0 / math.sqrt(HEAD)

    def one_head(head):
        low = (head * HEAD).astype(jnp.int32)
        qhead = lax.dynamic_slice_in_dim(queries, low, HEAD, 1).astype(jnp.float32)
        khead = lax.dynamic_slice_in_dim(keys, low, HEAD, 1).astype(jnp.float32)
        vhead = lax.dynamic_slice_in_dim(values, low, HEAD, 1).astype(jnp.float32)
        qmark = lax.dynamic_slice_in_dim(query_anchors, low, HEAD, 1)
        kmark = lax.dynamic_slice_in_dim(key_anchors, low, HEAD, 1)
        nearby_scores = jax.nn.softmax(jnp.dot(qhead, kmark.T, precision=HIGH_ACCURACY) * score_scale, axis=-1)
        anchor_block = jax.nn.softmax(jnp.dot(qmark, kmark.T, precision=HIGH_ACCURACY) * score_scale, axis=-1)
        distant_scores = jnp.dot(qmark, khead.T, precision=HIGH_ACCURACY) * score_scale
        peak = lax.optimization_barrier(jnp.max(distant_scores, axis=-1, keepdims=True))
        layer_weights = jnp.exp(distant_scores - peak)
        mass = lax.optimization_barrier(jnp.sum(layer_weights, axis=-1, keepdims=True))
        collected_rows = jnp.dot(layer_weights, vhead, precision=HIGH_ACCURACY) / mass
        token_mixer = jnp.dot(inverse_rounds(anchor_block), collected_rows, precision=HIGH_ACCURACY)
        return jnp.dot(nearby_scores, token_mixer, precision=HIGH_ACCURACY)
    heads_out = lax.map(one_head, jnp.arange(HEADS, dtype=jnp.int32))
    attn = jnp.transpose(heads_out, (1, 0, 2)).reshape(TOKENS, D).astype(jnp.bfloat16)
    group = D // N_MP
    proj = jnp.zeros((TOKENS, D), jnp.float32)
    for index in range(N_MP):
        part = jnp.dot(attn[:, index * group:(index + 1) * group], w_out[index * group:(index + 1) * group], preferred_element_type=jnp.float32)
        proj = proj + lax.optimization_barrier(part.astype(jnp.bfloat16)).astype(jnp.float32)
    resid = (stream.astype(jnp.float32) + proj).astype(jnp.bfloat16)
    resid32 = resid.astype(jnp.float32)
    meansq = lax.optimization_barrier(jnp.mean(resid32 * resid32, axis=-1, keepdims=True))
    normed = (resid32 * lax.rsqrt(meansq + EPS) * gain[None, :]).astype(jnp.bfloat16)
    share = FF // N_MP
    ffn = jnp.zeros((TOKENS, D), jnp.float32)
    for index in range(N_MP):
        gate = jnp.dot(normed, w_gate[:, index * share:(index + 1) * share], preferred_element_type=jnp.float32)
        upper = jnp.dot(normed, w_up[:, index * share:(index + 1) * share], preferred_element_type=jnp.float32)
        hidden = (jax.nn.silu(gate) * upper).astype(jnp.bfloat16)
        part = jnp.dot(hidden, w_down[index * share:(index + 1) * share], preferred_element_type=jnp.float32)
        ffn = ffn + lax.optimization_barrier(part.astype(jnp.bfloat16)).astype(jnp.float32)
    return (resid32 + ffn).astype(jnp.bfloat16)
```

```python
import math

import jax
import jax.numpy as jnp
from jax import lax
from jax.sharding import Mesh, PartitionSpec as P

PINV_ITERS = 6
HEAD = 128


HIGH_ACCURACY = lax.Precision.HIGHEST
EPS = 1e-05


def inverse_rounds(anchor_block):
    eye = jnp.eye(anchor_block.shape[-1], dtype=jnp.float32)
    col_most = jnp.max(jnp.sum(anchor_block, axis=1), axis=-1)
    row_most = jnp.max(jnp.sum(anchor_block, axis=2), axis=-1)
    approx = jnp.swapaxes(anchor_block, 1, 2) / (col_most * row_most)[:, None, None]
    for step in range(PINV_ITERS):
        prod = jnp.einsum("hij,hjk->hik", anchor_block, approx, precision=HIGH_ACCURACY)
        inner = 7.0 * eye - prod
        inner = 15.0 * eye - jnp.einsum("hij,hjk->hik", prod, inner, precision=HIGH_ACCURACY)
        inner = 13.0 * eye - jnp.einsum("hij,hjk->hik", prod, inner, precision=HIGH_ACCURACY)
        approx = 0.25 * jnp.einsum("hij,hjk->hik", approx, inner, precision=HIGH_ACCURACY)
    return approx


SEQ_AXES = ("z", "y", "c")


def seq_psum(x):
    for ax in reversed(SEQ_AXES):
        x = lax.psum(x, ax)
    return x


def seq_pmax(x):
    for ax in reversed(SEQ_AXES):
        x = lax.pmax(x, ax)
    return x


def seq_gather(x, axis):
    for ax in reversed(SEQ_AXES):
        x = lax.all_gather(x, ax, axis=axis, tiled=True)
    return x


def seq_index():
    idx = lax.axis_index(SEQ_AXES[0])
    for ax in SEQ_AXES[1:]:
        idx = idx * lax.axis_size(ax) + lax.axis_index(ax)
    return idx


def on_device(queries, keys, values, stream, seg_lengths, gain, w_out, w_gate, w_up, w_down):
    tok = queries.shape[0]
    width = queries.shape[1]
    heads = width // HEAD
    marks = seg_lengths.shape[0]
    score_scale = 1.0 / math.sqrt(HEAD)
    ends = jnp.cumsum(seg_lengths)
    starts = ends - seg_lengths
    place = seq_index() * tok + jnp.arange(tok, dtype=jnp.int32)
    member = ((place[:, None] >= starts[None, :]) & (place[:, None] < ends[None, :])).astype(
        jnp.bfloat16
    )
    query_part = jnp.dot(member.T, queries, preferred_element_type=jnp.float32)
    key_part = jnp.dot(member.T, keys, preferred_element_type=jnp.float32)
    query_sum, key_sum = seq_psum((query_part, key_part))
    counts = seg_lengths.astype(jnp.float32)[:, None]
    query_anchors = (query_sum / counts).reshape(marks, heads, HEAD)
    key_anchors = (key_sum / counts).reshape(marks, heads, HEAD)
    query_slice = queries.astype(jnp.float32).reshape(tok, heads, HEAD)
    key_slice = keys.astype(jnp.float32).reshape(tok, heads, HEAD)
    value_slice = values.astype(jnp.float32).reshape(tok, heads, HEAD)
    nearby_scores = jax.nn.softmax(
        jnp.einsum("brc,xrc->rbx", query_slice, key_anchors, precision=HIGH_ACCURACY) * score_scale,
        axis=-1,
    )
    anchor_block = jax.nn.softmax(
        jnp.einsum("oqc,bqc->qob", query_anchors, key_anchors, precision=HIGH_ACCURACY)
        * score_scale,
        axis=-1,
    )
    distant_scores = (
        jnp.einsum("gvb,lvb->vgl", query_anchors, key_slice, precision=HIGH_ACCURACY) * score_scale
    )
    local_peak = jnp.max(distant_scores, axis=-1)
    peak = seq_pmax(local_peak)
    layer_weights = jnp.exp(distant_scores - peak[..., None])
    local_mass = jnp.sum(layer_weights, axis=-1)
    slice_sum = jnp.einsum("vqb,bvn->vqn", layer_weights, value_slice, precision=HIGH_ACCURACY)
    mass, weighted = seq_psum((local_mass, slice_sum))
    collected_rows = weighted / mass[..., None]
    token_mixer = jnp.einsum(
        "svy,syc->svc", inverse_rounds(anchor_block), collected_rows, precision=HIGH_ACCURACY
    )
    attn = (
        jnp.einsum("ljz,lzx->jlx", nearby_scores, token_mixer, precision=HIGH_ACCURACY)
        .reshape(tok, width)
        .astype(jnp.bfloat16)
    )
    full_out = seq_gather(w_out, 1)
    out_terms = jnp.dot(attn, full_out, preferred_element_type=jnp.float32)
    proj = lax.psum_scatter(
        out_terms.astype(jnp.bfloat16), "mp", scatter_dimension=1, tiled=True
    ).astype(jnp.float32)
    resid = (stream.astype(jnp.float32) + proj).astype(jnp.bfloat16)
    whole = lax.all_gather(resid, "mp", axis=1, tiled=True)
    whole32 = whole.astype(jnp.float32)
    meansq = jnp.mean(whole32 * whole32, axis=-1, keepdims=True)
    normed = (whole32 * lax.rsqrt(meansq + EPS) * gain[None, :]).astype(jnp.bfloat16)
    full_gate, full_up = (
        seq_gather(w_gate, 0),
        seq_gather(w_up, 0),
    )
    gate = jnp.dot(normed, full_gate, preferred_element_type=jnp.float32)
    upper = jnp.dot(normed, full_up, preferred_element_type=jnp.float32)
    hidden = (jax.nn.silu(gate) * upper).astype(jnp.bfloat16)
    full_down = seq_gather(w_down, 1)
    down_terms = jnp.dot(hidden, full_down, preferred_element_type=jnp.float32)
    ffn = lax.psum_scatter(
        down_terms.astype(jnp.bfloat16), "mp", scatter_dimension=1, tiled=True
    ).astype(jnp.float32)
    return (resid.astype(jnp.float32) + ffn).astype(jnp.bfloat16)


def split_mesh(mesh):
    n_seq = mesh.shape["seq"]
    n_mp = mesh.shape["mp"]
    devs = mesh.devices.reshape(n_seq // 8, 4, 2, n_mp)
    return Mesh(devs, SEQ_AXES + ("mp",))


def solution(mesh):
    fine = split_mesh(mesh)
    S = SEQ_AXES
    return jax.shard_map(
        on_device,
        mesh=fine,
        in_specs=(
            P(S, "mp"),
            P(S, "mp"),
            P(S, "mp"),
            P(S, "mp"),
            P(),
            P(),
            P("mp", S),
            P(S, "mp"),
            P(S, "mp"),
            P("mp", S),
        ),
        out_specs=P(S, "mp"),
        check_vma=False,
    )
```
